32 devices in a mesh: seq: 8 (over z, x), head: 4 (over y, core).
Axes of the slice: x: 2, y: 2, z: 4, core: 2. Of those that a mesh axis runs over, the one named last changes fastest.
Arguments:
- block_input: bfloat16 [1, 4096, 2048], P(None, 'seq'), may hold values from -6 to 6
- decay_log: float32 [1, 4096, 8], P(None, 'seq', 'head'), as said below
- ln1_gain: float32 [2048], replicated, may hold values from 0.25 to 1.75
- w_query: bfloat16 [2048, 2048], P(None, 'head'), may hold values from -0.125 to 0.125
- w_key: bfloat16 [2048, 2048], P(None, 'head'), may hold values from -0.125 to 0.125
- w_value: bfloat16 [2048, 4096], P(None, 'head'), may hold values from -0.125 to 0.125
- w_swish: bfloat16 [2048, 4096], P(None, 'head'), may hold values from -0.125 to 0.125
- group_gain: float32 [8, 512], P('head'), may hold values from 0.25 to 1.75
- w_out: bfloat16 [4096, 2048], P('head'), may hold values from -0.1875 to 0.1875
- ln2_gain: float32 [2048], replicated, may hold values from 0.25 to 1.75
- w_mlp_gate: bfloat16 [2048, 4096], P(None, 'head'), may hold values from -0.125 to 0.125
- w_mlp_up: bfloat16 [2048, 4096], P(None, 'head'), may hold values from -0.125 to 0.125
- w_mlp_down: bfloat16 [4096, 2048], P('head'), may hold values from -0.1875 to 0.1875
- cotangent: bfloat16 [1, 4096, 2048], P(None, 'seq'), may hold values from -6 to 6
Outputs:
- block_output: float32 [1, 4096, 2048], P(None, 'seq')
- grad_input: float32 [1, 4096, 2048], P(None, 'seq')
- grad_ln1_gain: float32 [2048], P('seq')
- grad_w_query: float32 [2048, 2048], P('seq', 'head')
- grad_w_key: float32 [2048, 2048], P('seq', 'head')
- grad_w_value: float32 [2048, 4096], P('seq', 'head')
- grad_w_swish: float32 [2048, 4096], P('seq', 'head')
- grad_group_gain: float32 [8, 512], P('head', 'seq')
- grad_w_out: float32 [4096, 2048], P('head', 'seq')
- grad_ln2_gain: float32 [2048], P('seq')
- grad_w_mlp_gate: float32 [2048, 4096], P('seq', 'head')
- grad_w_mlp_up: float32 [2048, 4096], P('seq', 'head')
- grad_w_mlp_down: float32 [4096, 2048], P('head', 'seq')
The draws below stay inside these ranges and needn't reach their ends.
Inputs may be any that keep to these rules, and one draw needn't show every extreme that they name: `decay_log`: every entry is below zero.
All inputs are finite; a program needn't handle non-finite values.
Results may differ from the reference program's by a relative error of at most 0.03.
Values may be sent and summed in bfloat16 or wider, within the bound.
No kernel may reach another device: no remote copies, remote signals or barrier semaphores. Data moves between devices by JAX's collectives and lax.ppermute only.
A program may use at most 192 MiB of HBM per device.

```python
import math
import jax
import jax.numpy as jnp
from jax import lax

D = 2048
HEADS = 8
DK = 256
DV = 512
FF = 4096
SEQUENCE_COUNT = 1
SPAN = 512
SEQUENCE_LENGTH = 4096
N_HEAD = 4


def draw_decay_log(key, part):
    segment_parts = jax.random.split(key, 7)
    head_order = jax.random.permutation(segment_parts[0], HEADS)
    fast_heads = head_order < HEADS // 2
    slow_rate = jax.random.uniform(segment_parts[1], (HEADS,), jnp.float32, 0.05, 0.3) / SEQUENCE_LENGTH
    fast_rate = jax.random.uniform(segment_parts[2], (HEADS,), jnp.float32, 1.0 / 50.0, 1.0 / 30.0)
    baseline_decay_rate = jnp.where(fast_heads, fast_rate, slow_rate)
    noise_level = jax.random.uniform(segment_parts[3], (SEQUENCE_COUNT, SEQUENCE_LENGTH, HEADS), jnp.float32, 0.25, 1.75)
    block_decay_factor = jnp.exp(jax.random.uniform(segment_parts[4], (SEQUENCE_COUNT, SEQUENCE_LENGTH // SPAN, 1, HEADS), jnp.float32, -0.7, 0.7))
    block_decay_factor = jnp.broadcast_to(block_decay_factor, (SEQUENCE_COUNT, SEQUENCE_LENGTH // SPAN, SPAN, HEADS)).reshape(SEQUENCE_COUNT, SEQUENCE_LENGTH, HEADS)
    spike_position = jax.random.randint(segment_parts[5], (SEQUENCE_COUNT, 1, 3), 0, SEQUENCE_LENGTH)
    position_indices = jnp.arange(SEQUENCE_LENGTH, dtype=jnp.int32)[None, :, None]
    spike_triggered = jnp.any(position_indices == spike_position, axis=-1).astype(jnp.float32)
    spike_loss_term = jax.random.uniform(segment_parts[6], (SEQUENCE_COUNT, SEQUENCE_LENGTH), jnp.float32, math.log(0.5), math.log(0.8))
    return -(baseline_decay_rate * noise_level * block_decay_factor) + (spike_triggered * spike_loss_term)[:, :, None]


def strengthened(drawn, own_key, source, target, blocks, factor):
    def block_of(dim):
        return (jnp.arange(drawn.shape[dim]) // (drawn.shape[dim] // blocks)).reshape((-1,) + (1,) * (drawn.ndim - 1 - dim))

    near = jax.random.permutation(own_key, blocks)[block_of(target)]
    other_side = (block_of(target) + blocks // 2) % blocks
    return jnp.where((block_of(source) == near) | (block_of(source) == other_side), factor * drawn, drawn)


def steps_of(rng, dims, pieces, smallest, high):
    def one(axis_at, parts):
        heights = jax.random.uniform(jax.random.fold_in(jax.random.fold_in(rng, 6), axis_at), (parts,), jnp.float32, smallest / len(pieces), high / len(pieces))
        return jnp.repeat(jnp.exp(heights), dims[axis_at] // parts).reshape((-1,) + (1,) * (len(dims) - axis_at - 1))

    level = one(*pieces[0])
    for cut in pieces[1:]:
        level = level * one(*cut)
    return level


def scatter_about(stream_key, dims, deviation, most, shards=(), held_as=jnp.bfloat16):
    factor_of = steps_of(stream_key, dims, shards, -0.22, 0.18) if shards else 1.0
    entries = jax.random.normal(stream_key, dims, jnp.float32) * deviation * factor_of
    return jnp.minimum(jnp.maximum(entries, -most), most).astype(held_as)


def bell_draw_with(key, dims, width, bound, cuts, heavy, held_as=jnp.bfloat16):
    entries = width * jax.random.normal(key, dims, jnp.float32)
    if cuts:
        entries = entries * steps_of(key, dims, cuts, -0.22, 0.18)
    return jnp.clip(strengthened(entries, jax.random.fold_in(key, 3), *heavy), -bound, bound).astype(held_as)


def setup_inputs(seed: int = 0) -> dict:
    streams_of = jax.random.split(jax.random.key(seed), 15)
    return {
        "block_input": scatter_about(streams_of[0], (SEQUENCE_COUNT, SEQUENCE_LENGTH, D), 1.0, 6.0, ((1, 8),)),
        "decay_log": draw_decay_log(jax.random.fold_in(streams_of[14], 71), 0),
        "ln1_gain": jnp.clip(1.0 + 0.15 * jax.random.normal(streams_of[2], (D,), jnp.float32), 0.25, 1.75),
        "w_query": scatter_about(streams_of[3], (D, HEADS * DK), D ** -0.5, 0.125, ((1, 4),)),
        "w_key": scatter_about(streams_of[4], (D, HEADS * DK), D ** -0.5, 0.125, ((1, 4),)),
        "w_value": scatter_about(streams_of[5], (D, HEADS * DV), D ** -0.5, 0.125, ((1, 4),)),
        "w_swish": scatter_about(streams_of[6], (D, HEADS * DV), D ** -0.5, 0.125, ((1, 4),)),
        "group_gain": jnp.clip(1.0 + 0.15 * jax.random.normal(streams_of[7], (HEADS, DV), jnp.float32), 0.25, 1.75),
        "w_out": scatter_about(streams_of[8], (HEADS * DV, D), (HEADS * DV // 4) ** -0.5, 0.1875, ((0, 4),)),
        "ln2_gain": jnp.clip(1.0 + 0.15 * jax.random.normal(streams_of[9], (D,), jnp.float32), 0.25, 1.75),
        "w_mlp_gate": scatter_about(streams_of[10], (D, FF), D ** -0.5, 0.125, ((1, 4),)),
        "w_mlp_up": scatter_about(streams_of[11], (D, FF), D ** -0.5, 0.125, ((1, 4),)),
        "w_mlp_down": scatter_about(streams_of[12], (FF, D), (FF // 4) ** -0.5, 0.1875, ((0, 4),)),
        "cotangent": bell_draw_with(streams_of[13], (SEQUENCE_COUNT, SEQUENCE_LENGTH, D), 1.0, 6.0, ((1, 8),), (1, 2, 8, 2.0)),
    }


NORM_EPS = 1e-05

def float32_result(array_in):
    return array_in.astype(jnp.float32)

def narrow(array_in):
    return lax.optimization_barrier(array_in.astype(jnp.bfloat16))

def norm_rows(row_data):
    row_mean = lax.optimization_barrier(jnp.mean(row_data, axis=-1, keepdims=True))
    centered = row_data - row_mean
    inv_std = lax.rsqrt(lax.optimization_barrier(jnp.mean(centered * centered, axis=-1, keepdims=True)) + NORM_EPS)
    return (centered * inv_std, inv_std)

def norm_back(grad_in, normed, inv_std):
    return inv_std * (grad_in - lax.optimization_barrier(jnp.mean(grad_in, axis=-1, keepdims=True)) - normed * lax.optimization_barrier(jnp.mean(grad_in * normed, axis=-1, keepdims=True)))

def swish_parts(pre_act):
    sig_val = jax.nn.sigmoid(pre_act)
    return (pre_act * sig_val, sig_val * (1.0 + pre_act * (1.0 - sig_val)))

def group_sum(pairs):
    row_count = pairs[0][0].shape[0]
    out_width = pairs[0][1].shape[1]

    def add_group(accum, group_index):
        partial_sum = jnp.zeros((row_count, out_width), jnp.float32)
        for left_op, right_op in pairs:
            group_width = left_op.shape[1] // N_HEAD
            start_at = (group_index * group_width).astype(jnp.int32)
            left_slice = lax.dynamic_slice_in_dim(left_op, start_at, group_width, 1)
            right_slice = lax.dynamic_slice_in_dim(right_op, start_at, group_width, 0)
            partial_sum = partial_sum + jnp.dot(left_slice, right_slice, preferred_element_type=jnp.float32)
        return (accum + float32_result(narrow(partial_sum)), None)
    start_sum = jnp.zeros((row_count, out_width), jnp.float32)
    return lax.scan(add_group, start_sum, jnp.arange(N_HEAD, dtype=jnp.int32))[0]

def decay_terms(decays):
    cumulative_decay = jnp.cumsum(decays, axis=0)
    block_total = cumulative_decay[-1]
    per_head = cumulative_decay.T
    block_len = decays.shape[0]
    causal = lax.broadcasted_iota(jnp.int32, (block_len, block_len), 0) >= lax.broadcasted_iota(jnp.int32, (block_len, block_len), 1)
    gap_log = jnp.minimum(per_head[:, :, None] - per_head[:, None, :], 0.0)
    weight = jnp.where(causal[None], jnp.exp(gap_log), 0.0)
    return (cumulative_decay, block_total, weight)

def block_forward(state_in, inputs):
    query_matrix, key_matrix_rows, content_array, decays = inputs
    cumulative_decay, block_total, weight = decay_terms(decays)
    scores = jnp.einsum('thk,shk->hts', float32_result(query_matrix), float32_result(key_matrix_rows))
    affinity_table = narrow(scores * weight)
    query_decay_weights = narrow(float32_result(query_matrix) * jnp.exp(cumulative_decay)[:, :, None])
    lookup_fading_coefficients = narrow(float32_result(key_matrix_rows) * jnp.exp(block_total[None, :] - cumulative_decay)[:, :, None])
    block_local_state = jnp.einsum('dmf,dmx->mfx', float32_result(lookup_fading_coefficients), float32_result(content_array))
    state_half_precision = narrow(state_in)
    retention_output = jnp.einsum('wia,awn->iwn', float32_result(affinity_table), float32_result(content_array)) + jnp.einsum('xju,jua->xja', float32_result(query_decay_weights), float32_result(state_half_precision))
    state_next = jnp.exp(block_total)[:, None, None] * state_in + block_local_state
    return (state_next, (retention_output, state_in))

def block_backward(state_grad, inputs):
    query_matrix, key_matrix_rows, content_array, decays, memory_derivative, state_in = inputs
    cumulative_decay, block_total, weight = decay_terms(decays)
    scores = jnp.einsum('thk,shk->hts', float32_result(query_matrix), float32_result(key_matrix_rows))
    affinity_table = narrow(scores * weight)
    query_decay_weights = narrow(float32_result(query_matrix) * jnp.exp(cumulative_decay)[:, :, None])
    key_scale_factor = jnp.exp(block_total[None, :] - cumulative_decay)
    lookup_fading_coefficients = narrow(float32_result(key_matrix_rows) * key_scale_factor[:, :, None])
    state_half_precision = narrow(state_in)
    derivative_bf16 = narrow(state_grad)
    score_gradient = narrow(jnp.einsum('thv,shv->hts', float32_result(memory_derivative), float32_result(content_array)) * weight)
    query_gradient_rows = jnp.einsum('gzm,mgi->zgi', float32_result(score_gradient), float32_result(key_matrix_rows)) + jnp.exp(cumulative_decay)[:, :, None] * jnp.einsum('dmx,mrx->dmr', float32_result(memory_derivative), float32_result(state_half_precision))
    key_gradient_rows = jnp.einsum('nva,vnf->anf', float32_result(score_gradient), float32_result(query_matrix)) + key_scale_factor[:, :, None] * jnp.einsum('izn,zpn->izp', float32_result(content_array), float32_result(derivative_bf16))
    content_derivative_lines = jnp.einsum('yds,dyx->syx', float32_result(affinity_table), float32_result(memory_derivative)) + jnp.einsum('ytm,tma->yta', float32_result(lookup_fading_coefficients), float32_result(derivative_bf16))
    block_local_gradient = jnp.einsum('olj,ola->lja', float32_result(query_decay_weights), float32_result(memory_derivative))
    carry_out = jnp.exp(block_total)[:, None, None] * state_grad + block_local_gradient
    return (carry_out, (narrow(query_gradient_rows), narrow(key_gradient_rows), narrow(content_derivative_lines)))

def one_sequence(inputs_row, decays, cot_rows, weights):
    ln1_gain, w_query, w_key, w_value, w_swish, group_gain, w_out, ln2_gain, w_mlp_gate, w_mlp_up, w_mlp_down = weights
    length = inputs_row.shape[0]
    blocks = length // SPAN
    source = float32_result(inputs_row)
    normed_one, inv_one = norm_rows(source)
    normed_bf = narrow(normed_one * ln1_gain)
    query_matrix = narrow(jnp.dot(normed_bf, w_query, preferred_element_type=jnp.float32))
    key_matrix_rows = narrow(jnp.dot(normed_bf, w_key, preferred_element_type=jnp.float32))
    content_array = narrow(jnp.dot(normed_bf, w_value, preferred_element_type=jnp.float32))
    swish_pre = jnp.dot(normed_bf, w_swish, preferred_element_type=jnp.float32)
    query_blocks = query_matrix.reshape(blocks, SPAN, HEADS, DK)
    key_blocks = key_matrix_rows.reshape(blocks, SPAN, HEADS, DK)
    value_blocks = content_array.reshape(blocks, SPAN, HEADS, DV)
    decay_blocks = decays.reshape(blocks, SPAN, HEADS)
    zero_state = jnp.zeros((HEADS, DK, DV), jnp.float32)
    unused, (ret_blocks, state_ins) = lax.scan(block_forward, zero_state, (query_blocks, key_blocks, value_blocks, decay_blocks))
    retention_output = ret_blocks.reshape(length, HEADS, DV)
    ret_hat, ret_inv = norm_rows(retention_output)
    swish_val, swish_grad = swish_parts(swish_pre)
    scaled = (ret_hat * group_gain).reshape(length, HEADS * DV)
    gated_rows = narrow(swish_val * scaled)
    attended = group_sum([(gated_rows, w_out)])
    resid_one = source + attended
    normed_two, inv_two = norm_rows(resid_one)
    mlp_in = narrow(normed_two * ln2_gain)
    mlp_gate = jnp.dot(mlp_in, w_mlp_gate, preferred_element_type=jnp.float32)
    mlp_up = jnp.dot(mlp_in, w_mlp_up, preferred_element_type=jnp.float32)
    mlp_silu, mlp_dsilu = swish_parts(mlp_gate)
    mlp_hidden = narrow(mlp_silu * mlp_up)
    mlp_out = group_sum([(mlp_hidden, w_mlp_down)])
    block_output = resid_one + mlp_out
    grad_hidden = jnp.dot(cot_rows, w_mlp_down.T, preferred_element_type=jnp.float32)
    grad_mgate = narrow(grad_hidden * mlp_up * mlp_dsilu)
    grad_mup = narrow(grad_hidden * mlp_silu)
    grad_down = jnp.dot(mlp_hidden.T, cot_rows, preferred_element_type=jnp.float32)
    grad_mlp_gate = jnp.dot(mlp_in.T, grad_mgate, preferred_element_type=jnp.float32)
    grad_mlp_up = jnp.dot(mlp_in.T, grad_mup, preferred_element_type=jnp.float32)
    grad_norm_two = group_sum([(grad_mgate, w_mlp_gate.T), (grad_mup, w_mlp_up.T)])
    grad_ln2 = lax.optimization_barrier(jnp.sum(grad_norm_two * normed_two, axis=0))
    grad_resid = float32_result(cot_rows) + norm_back(grad_norm_two * ln2_gain, normed_two, inv_two)
    grad_resid_bf = narrow(grad_resid)
    grad_out = jnp.dot(gated_rows.T, grad_resid_bf, preferred_element_type=jnp.float32)
    grad_gated = jnp.dot(grad_resid_bf, w_out.T, preferred_element_type=jnp.float32)
    grad_swish = narrow(grad_gated * scaled * swish_grad)
    grad_scaled = (grad_gated * swish_val).reshape(length, HEADS, DV)
    grad_group = lax.optimization_barrier(jnp.sum(grad_scaled * ret_hat, axis=0))
    memory_derivative = narrow(norm_back(grad_scaled * group_gain, ret_hat, ret_inv))
    grad_blocks = memory_derivative.reshape(blocks, SPAN, HEADS, DV)
    unused_grad, (grad_q, grad_k, grad_v) = lax.scan(block_backward, zero_state, (query_blocks, key_blocks, value_blocks, decay_blocks, grad_blocks, state_ins), reverse=True)
    grad_queries = grad_q.reshape(length, HEADS * DK)
    grad_keys = grad_k.reshape(length, HEADS * DK)
    grad_values = grad_v.reshape(length, HEADS * DV)
    grad_wq = jnp.dot(normed_bf.T, grad_queries, preferred_element_type=jnp.float32)
    grad_wk = jnp.dot(normed_bf.T, grad_keys, preferred_element_type=jnp.float32)
    grad_wv = jnp.dot(normed_bf.T, grad_values, preferred_element_type=jnp.float32)
    grad_wsw = jnp.dot(normed_bf.T, grad_swish, preferred_element_type=jnp.float32)
    grad_norm_one = group_sum([(grad_queries, w_query.T), (grad_keys, w_key.T), (grad_values, w_value.T), (grad_swish, w_swish.T)])
    grad_ln1 = lax.optimization_barrier(jnp.sum(grad_norm_one * normed_one, axis=0))
    grad_input = grad_resid + norm_back(grad_norm_one * ln1_gain, normed_one, inv_one)
    grads = (grad_ln1, grad_wq, grad_wk, grad_wv, grad_wsw, grad_group, grad_out, grad_ln2, grad_mlp_gate, grad_mlp_up, grad_down)
    return (block_output, grad_input, grads)

def reference(block_input, decay_log, ln1_gain, w_query, w_key, w_value, w_swish, group_gain, w_out, ln2_gain, w_mlp_gate, w_mlp_up, w_mlp_down, cotangent):
    weights = (ln1_gain, w_query, w_key, w_value, w_swish, group_gain, w_out, ln2_gain, w_mlp_gate, w_mlp_up, w_mlp_down)
    outputs = []
    input_grads = []
    totals = (jnp.zeros((D,), jnp.float32), jnp.zeros((D, HEADS * DK), jnp.float32), jnp.zeros((D, HEADS * DK), jnp.float32), jnp.zeros((D, HEADS * DV), jnp.float32), jnp.zeros((D, HEADS * DV), jnp.float32), jnp.zeros((HEADS, DV), jnp.float32), jnp.zeros((HEADS * DV, D), jnp.float32), jnp.zeros((D,), jnp.float32), jnp.zeros((D, FF), jnp.float32), jnp.zeros((D, FF), jnp.float32), jnp.zeros((FF, D), jnp.float32))
    for seq_index in range(SEQUENCE_COUNT):
        block_output, grad_input, grads = one_sequence(block_input[seq_index], decay_log[seq_index], cotangent[seq_index], weights)
        outputs.append(block_output)
        input_grads.append(grad_input)
        totals = jax.tree.map(lambda acc_val, new_val: acc_val + new_val, totals, grads)
    return (jnp.stack(outputs), jnp.stack(input_grads), totals[0], totals[1], totals[2], totals[3], totals[4], totals[5], totals[6], totals[7], totals[8], totals[9], totals[10])
```

```python
import jax
import jax.numpy as jnp
from jax import lax
from jax.sharding import PartitionSpec as P

NORM_EPS = 1e-05
f32 = jnp.float32
bf16 = jnp.bfloat16


def mat_prod(left_op, right_op):
    return jnp.dot(left_op, right_op, preferred_element_type=f32)


def mat_right_t(left_op, right_op):
    return lax.dot_general(left_op, right_op, (((1,), (1,)), ((), ())), preferred_element_type=f32)


def mat_left_t(left_op, right_op):
    return lax.dot_general(left_op, right_op, (((0,), (0,)), ((), ())), preferred_element_type=f32)


def norm_rows(row_data):
    row_mean = jnp.mean(row_data, axis=-1, keepdims=True)
    centered = row_data - row_mean
    inv_std = lax.rsqrt(jnp.mean(centered * centered, axis=-1, keepdims=True) + NORM_EPS)
    return (centered * inv_std, inv_std)


def norm_back(grad_in, normed, inv_std):
    return inv_std * (
        grad_in
        - jnp.mean(grad_in, axis=-1, keepdims=True)
        - normed * jnp.mean(grad_in * normed, axis=-1, keepdims=True)
    )


def swish_parts(pre_act):
    sig_val = jax.nn.sigmoid(pre_act)
    return (pre_act * sig_val, sig_val * (1.0 + pre_act * (1.0 - sig_val)))


def bits_of(axis):
    size = lax.axis_size(axis)
    bits = size.bit_length() - 1
    if size != 1 << bits:
        raise ValueError("axis size")
    return bits


def flip(x, axis, bit):
    return lax.ppermute(x, axis, [(i, i ^ (1 << bit)) for i in range(lax.axis_size(axis))])


def half_of(x, which, dim):
    size = x.shape[dim] // 2
    return lax.dynamic_slice_in_dim(x, which * size, size, dim)


def swap_halves(x, flag, dim=0):
    low, high = jnp.split(x, 2, axis=dim)
    return jnp.where(flag == 0, x, jnp.concatenate([high, low], axis=dim))


def both_halves(own):
    return jnp.concatenate([own, flip(own, "head", 0)], axis=0)


def sum_over_head(partial):
    own, other = jnp.split(partial, 2, axis=0)
    total = own.astype(f32) + flip(other, "head", 0).astype(f32)
    for bit in range(1, bits_of("head")):
        total = total + flip(total.astype(bf16), "head", bit).astype(f32)
    return total


def entering_state(local, decay, reverse):
    size = lax.axis_size("seq")
    if size == 1:
        return jnp.zeros_like(local)
    me = lax.axis_index("seq")
    pair, odd = me // 2, me % 2
    late = 1 - odd if reverse else odd
    decay_other = flip(decay, "seq", 0)
    dec = decay[:, :, None, None]
    dec_other = decay_other[:, :, None, None]
    mine = half_of(local, odd, 2)
    theirs = flip(half_of(local, 1 - odd, 2).astype(bf16), "seq", 0).astype(f32)
    first = late == 0
    total = jnp.where(first, dec_other * mine + theirs, dec * theirs + mine)
    both = dec * dec_other
    carry = jnp.zeros_like(total)
    pairs = size // 2
    for hop in range(pairs - 1):
        source = pairs - 1 - hop if reverse else hop
        target = source - 1 if reverse else source + 1
        links = [(2 * source + o, 2 * target + o) for o in range(2)]
        moved = lax.ppermute((both * carry + total).astype(bf16), "seq", links)
        carry = carry + moved.astype(f32)
    to_other = jnp.where(first, dec * carry + mine, carry)
    own = jnp.where(first, carry, dec_other * carry + theirs)
    got = flip(to_other.astype(bf16), "seq", 0)
    own = own.astype(bf16)
    return jnp.where(
        odd == 0, jnp.concatenate([own, got], axis=2), jnp.concatenate([got, own], axis=2)
    )


def owner_masks(bits):
    order = [0]
    for bit in reversed(range(1, bits)):
        order = [m | (1 << bit) for m in order] + order
    return order


def owner_columns(full, device, masks, width):
    return jnp.concatenate(
        [lax.dynamic_slice_in_dim(full, (device ^ m) * width, width, 1) for m in masks], axis=1
    )


def shared_side(full, own_rows):
    bits = bits_of("seq")
    me = lax.axis_index("seq")
    width = full.shape[1] // lax.axis_size("seq")
    masks = owner_masks(bits)
    mine = owner_columns(full, me, masks, width)
    sent = owner_columns(own_rows, me ^ 1, masks, width)
    return mine, both_halves(flip(sent, "seq", 0))


def weight_grad(side, shared, d_first):
    mine, theirs = shared
    side_other = flip(side, "seq", 0)
    bits = bits_of("seq")
    width = mine.shape[1] >> (bits - 1)
    dim = 0 if d_first else 1

    def part(low, high):
        if d_first:
            return mat_left_t(mine[:, low:high], side) + mat_left_t(theirs[:, low:high], side_other)
        return mat_left_t(side, mine[:, low:high]) + mat_left_t(side_other, theirs[:, low:high])

    count = mine.shape[1]
    if bits == 1:
        return part(0, count)
    sent = part(0, count // 2).astype(bf16)
    kept = lax.optimization_barrier(part(count // 2, count))
    for bit in range(1, bits):
        kept = kept + flip(sent, "seq", bit).astype(f32)
        if bit < bits - 1:
            away, kept = jnp.split(kept, 2, axis=dim)
            sent = away.astype(bf16)
    return kept


def small_sum(x):
    for bit in range(bits_of("seq")):
        x = x + flip(x, "seq", bit)
    return x


def own_block(x, dim):
    size = lax.axis_size("seq")
    width = x.shape[dim] // size
    return lax.dynamic_slice_in_dim(x, lax.axis_index("seq") * width, width, dim)


def body(
    block_input,
    decay_log,
    ln1_gain,
    w_query,
    w_key,
    w_value,
    w_swish,
    group_gain,
    w_out,
    ln2_gain,
    w_mlp_gate,
    w_mlp_up,
    w_mlp_down,
    cotangent,
):
    seq_count, block_len, model_dim = block_input.shape
    heads_here, value_dim = group_gain.shape
    key_dim = w_query.shape[1] // heads_here
    rows = seq_count * block_len
    own = block_len // 2
    core = lax.axis_index("head") % 2

    def heads(x, dim):
        return x.reshape(seq_count, block_len, heads_here, dim)

    x_rel = swap_halves(block_input, core, 1).reshape(rows, model_dim)
    cot = swap_halves(cotangent, core, 1).reshape(rows, model_dim)
    half_rows = rows // 2

    def own_half(x):
        return x[:half_rows]

    source = x_rel.astype(f32)
    normed_one, inv_one = norm_rows(source)
    normed_bf = (normed_one * ln1_gain).astype(bf16)
    keys_all = heads(mat_prod(normed_bf, w_key).astype(bf16), key_dim)
    content_array = heads(mat_prod(normed_bf, w_value).astype(bf16), value_dim)

    cumulative_true = jnp.cumsum(decay_log, axis=1)
    block_total = cumulative_true[:, -1, :]
    cumulative_decay = swap_halves(cumulative_true, core, 1)
    place = (lax.broadcasted_iota(jnp.int32, (block_len, block_len), 0) + core * own) % block_len
    place_s = (lax.broadcasted_iota(jnp.int32, (block_len, block_len), 1) + core * own) % block_len
    per_head = jnp.transpose(cumulative_decay, (0, 2, 1))
    gap_log = jnp.minimum(per_head[:, :, :, None] - per_head[:, :, None, :], 0.0)
    weight = jnp.where((place >= place_s)[None, None], jnp.exp(gap_log), 0.0)
    query_scale = jnp.exp(cumulative_decay)[:, :, :, None]
    key_scale = jnp.exp(block_total[:, None, :] - cumulative_decay)[:, :, :, None]
    decay_all = jnp.exp(block_total)

    key_dec = (keys_all.astype(f32) * key_scale).astype(bf16)
    local_state = jnp.einsum(
        "bshk,bshv->bhkv", key_dec, content_array, preferred_element_type=f32
    )
    state_bf = entering_state(local_state, decay_all, False)

    query_matrix = heads(mat_prod(normed_bf, w_query).astype(bf16), key_dim)
    swish_pre = mat_prod(normed_bf, w_swish)
    swish_val, swish_grad = swish_parts(swish_pre)
    scores = jnp.einsum("bthk,bshk->bhts", query_matrix, keys_all, preferred_element_type=f32)
    affinity = (scores * weight).astype(bf16)
    query_dec = (query_matrix.astype(f32) * query_scale).astype(bf16)
    inner = jnp.einsum("bhts,bshv->bthv", affinity, content_array, preferred_element_type=f32)
    grad_hidden = mat_right_t(cot, w_mlp_down)

    retained = inner + jnp.einsum(
        "bthk,bhkv->bthv", query_dec, state_bf, preferred_element_type=f32
    )
    ret_hat, ret_inv = norm_rows(retained)
    scaled = (ret_hat * group_gain).reshape(rows, heads_here * value_dim)
    gated_rows = (swish_val * scaled).astype(bf16)
    attended = sum_over_head(mat_prod(gated_rows, w_out).astype(bf16))

    resid_one = own_half(source) + attended
    normed_two, inv_two = norm_rows(resid_one)
    mlp_in_own = (normed_two * ln2_gain).astype(bf16)
    mlp_in = both_halves(mlp_in_own)
    mlp_gate = mat_prod(mlp_in, w_mlp_gate)
    mlp_up = mat_prod(mlp_in, w_mlp_up)
    mlp_silu, mlp_dsilu = swish_parts(mlp_gate)
    mlp_hidden = (mlp_silu * mlp_up).astype(bf16)
    grad_mgate = (grad_hidden * mlp_up * mlp_dsilu).astype(bf16)
    grad_mup = (grad_hidden * mlp_silu).astype(bf16)
    grad_norm_two = sum_over_head(
        (mat_right_t(grad_mgate, w_mlp_gate) + mat_right_t(grad_mup, w_mlp_up)).astype(bf16)
    )

    shared_cot = shared_side(cot, own_half(cot))
    shared_mlp = shared_side(mlp_in, mlp_in_own)
    shared_one = shared_side(normed_bf, own_half(normed_bf))
    grad_down = weight_grad(mlp_hidden, shared_cot, False)
    grad_gate_w = weight_grad(grad_mgate, shared_mlp, True)
    grad_up_w = weight_grad(grad_mup, shared_mlp, True)

    ln2_part = jnp.sum(grad_norm_two * normed_two, axis=0)
    grad_resid = own_half(cot).astype(f32) + norm_back(grad_norm_two * ln2_gain, normed_two, inv_two)
    grad_resid_own = grad_resid.astype(bf16)
    grad_resid_bf = both_halves(grad_resid_own)
    grad_gated = mat_right_t(grad_resid_bf, w_out)
    grad_swish = (grad_gated * scaled * swish_grad).astype(bf16)
    grad_scaled = heads(grad_gated * swish_val, value_dim)
    group_part = jnp.sum(grad_scaled * ret_hat, axis=(0, 1))
    grad_ret = norm_back(grad_scaled * group_gain, ret_hat, ret_inv).astype(bf16)
    local_grad = jnp.einsum("bthk,bthv->bhkv", query_dec, grad_ret, preferred_element_type=f32)
    state_grad = entering_state(local_grad, decay_all, True)

    mlp_out = sum_over_head(mat_prod(mlp_hidden, w_mlp_down).astype(bf16))
    block_output_own = resid_one + mlp_out

    shared_out = shared_side(grad_resid_bf, grad_resid_own)
    grad_out = weight_grad(gated_rows, shared_out, False)
    grad_wsw = weight_grad(grad_swish, shared_one, True)

    grad_score = (
        jnp.einsum("bthv,bshv->bhts", grad_ret, content_array, preferred_element_type=f32) * weight
    ).astype(bf16)
    grad_queries = (
        jnp.einsum("bhts,bshk->bthk", grad_score, keys_all, preferred_element_type=f32)
        + query_scale
        * jnp.einsum("bthv,bhkv->bthk", grad_ret, state_bf, preferred_element_type=f32)
    ).astype(bf16)
    grad_keys = (
        jnp.einsum("bhts,bthk->bshk", grad_score, query_matrix, preferred_element_type=f32)
        + key_scale
        * jnp.einsum("bshv,bhkv->bshk", content_array, state_grad, preferred_element_type=f32)
    ).astype(bf16)
    grad_values = (
        jnp.einsum("bhts,bthv->bshv", affinity, grad_ret, preferred_element_type=f32)
        + jnp.einsum("bshk,bhkv->bshv", key_dec, state_grad, preferred_element_type=f32)
    ).astype(bf16)
    grad_queries = grad_queries.reshape(rows, heads_here * key_dim)
    grad_keys = grad_keys.reshape(rows, heads_here * key_dim)
    grad_values = grad_values.reshape(rows, heads_here * value_dim)

    grad_wq = weight_grad(grad_queries, shared_one, True)
    grad_norm_one = sum_over_head(
        (
            mat_right_t(grad_swish, w_swish)
            + mat_right_t(grad_queries, w_query)
            + mat_right_t(grad_keys, w_key)
            + mat_right_t(grad_values, w_value)
        ).astype(bf16)
    )
    grad_wk = weight_grad(grad_keys, shared_one, True)
    grad_wv = weight_grad(grad_values, shared_one, True)
    ln1_part = jnp.sum(grad_norm_one * own_half(normed_one), axis=0)
    grad_input_own = grad_resid + norm_back(
        grad_norm_one * ln1_gain, own_half(normed_one), own_half(inv_one)
    )

    def gain_grad(part):
        return own_block(small_sum(part + flip(part, "head", 0)), 0)

    def rows_out(own_part):
        whole = both_halves(own_part).reshape(seq_count, block_len, model_dim)
        return swap_halves(whole, core, 1)

    return (
        rows_out(block_output_own),
        rows_out(grad_input_own),
        gain_grad(ln1_part),
        grad_wq,
        grad_wk,
        grad_wv,
        grad_wsw,
        own_block(small_sum(group_part), 1),
        grad_out,
        gain_grad(ln2_part),
        grad_gate_w,
        grad_up_w,
        grad_down,
    )


def solution(mesh):
    in_specs = (
        P(None, "seq", None),
        P(None, "seq", "head"),
        P(),
        P(None, "head"),
        P(None, "head"),
        P(None, "head"),
        P(None, "head"),
        P("head", None),
        P("head", None),
        P(),
        P(None, "head"),
        P(None, "head"),
        P("head", None),
        P(None, "seq", None),
    )
    out_specs = (
        P(None, "seq", None),
        P(None, "seq", None),
        P("seq"),
        P("seq", "head"),
        P("seq", "head"),
        P("seq", "head"),
        P("seq", "head"),
        P("head", "seq"),
        P("head", "seq"),
        P("seq"),
        P("seq", "head"),
        P("seq", "head"),
        P("head", "seq"),
    )
    return jax.shard_map(body, mesh=mesh, in_specs=in_specs, out_specs=out_specs, check_vma=False)
```
